128 devices in a mesh: slot: 32 (over y, x, core), own: 4 (over z).
Axes of the slice: x: 4, y: 4, z: 4, core: 2. Of those that a mesh axis runs over, the one named last changes fastest.
Arguments:
- slot_grads: bfloat16 [128, 768, 2048], P(('slot', 'own')), may hold values from -6 to 6
- weights: bfloat16 [64, 768, 2048], P(None, 'slot', 'own'), may hold values from -0.21875 to 0.21875
- moment: float32 [64, 768, 2048], P(None, 'slot', 'own'), may hold values from -2 to 2
- second: float32 [64, 768, 2048], P(None, 'slot', 'own'), may hold values from 0.01 to 1
- counts_old: int32 [64], replicated, may hold values from 1 to 4, as said below
- counts_new: int32 [64], replicated, may hold values from 1 to 4, as said below
- inputs: bfloat16 [32768, 768], P(('slot', 'own')), may hold values from -6 to 6
- row_slot: int32 [32768, 1], P(('slot', 'own')), may hold values from 0 to 127; in each aligned block of 256 rows (0 to 255, 256 to 511, ...) at most 4 rows name the same one
Outputs:
- new_weights: bfloat16 [64, 768, 2048], P(None, 'slot', 'own')
- new_moment: float32 [64, 768, 2048], P(None, 'slot', 'own')
- new_second: float32 [64, 768, 2048], P(None, 'slot', 'own')
- outputs: bfloat16 [32768, 2048], P(('slot', 'own'))
The draws below stay inside these ranges and needn't reach their ends.
Inputs may be any that keep to these rules, and one draw needn't show every extreme that they name: counts_old sums to 128; some expert has 4 replicas and some has 1. counts_new sums to 128; some expert has 4 replicas and some has 1. `row_slot`: the 256 rows of one device name any one slot at most 4 times, a bound that some block reaches.
All inputs are finite; a program needn't handle non-finite values.
Results may differ from the reference program's by a relative error of at most 0.0049.
Values may be sent and summed in bfloat16 or wider, within the bound.
No kernel may reach another device: no remote copies, remote signals or barrier semaphores. Data moves between devices by JAX's collectives and lax.ppermute only.
A program may use at most 128 MiB of HBM per device.

```python
import math
import jax
import jax.numpy as jnp
import numpy as np
from jax import lax

D = 2048
FF = 768
TOK_DEV = 256
SLOTS = 128
EXPERTS = 64
CAP = 4
TOKENS = 32768


def replica_counts(key):
    order = jax.random.permutation(key, EXPERTS)
    heavy = EXPERTS // 8
    light = EXPERTS // 4
    rest = EXPERTS - heavy - light
    swing = jax.random.randint(jax.random.fold_in(key, 7), (rest // 2,), -1, 2).astype(jnp.int32)
    ranked = jnp.concatenate([jnp.full((heavy,), 4, jnp.int32), jnp.full((light,), 1, jnp.int32), 2 + swing, 2 - swing])
    return jnp.zeros((EXPERTS,), jnp.int32).at[order].set(ranked)


def draw_counts_old(key, part):
    return replica_counts(jax.random.fold_in(key, 11))


def draw_counts_new(key, part):
    return replica_counts(jax.random.fold_in(key, 23))


def level_of(key, extent, pieces, least, largest):
    gain = 1.0
    for axis_at, shards_of in pieces:
        steps = jax.random.uniform(jax.random.fold_in(jax.random.fold_in(key, 6), axis_at), (shards_of,), jnp.float32, least / len(pieces), largest / len(pieces))
        gain = gain * jnp.repeat(jnp.exp(steps), extent[axis_at] // shards_of).reshape((-1,) + (1,) * (len(extent) - 1 - axis_at))
    return gain


def deal_out(stream_key, own, number, rows, count, top, most, lean):
    ranking = jax.random.permutation(stream_key, count)
    heavy_load, usual = load_shares(count, rows * top, most, lean, True), load_shares(count, rows * top, most, lean, False)
    places = jnp.arange(count)

    def named(lengths, turn):
        used = int((lengths > 0).sum())
        fixed = max(1, used // 4)
        moved = fixed + (places - fixed + turn * (used - fixed)) % max(1, count - fixed)
        return jnp.zeros((count,), jnp.int32).at[ranking[jnp.where(places < fixed, places, moved)]].set(jnp.asarray(lengths, jnp.int32))

    lengths = jnp.where(number % 4 == 0, named(heavy_load, number // 4), named(usual, number - number // 4 - 1))
    mixed = jax.random.permutation(jax.random.fold_in(own, 3), count)
    giver, sink = mixed[0:count // 2 * 2:2], mixed[1:count // 2 * 2:2]
    margin = jnp.minimum(lengths[giver] - 1, most - lengths[sink]) // 2
    margin = jnp.where((giver == ranking[0]) | (sink == ranking[0]) | (lengths[sink] == 0), 0, jnp.maximum(margin, 0))
    moved = jax.random.randint(jax.random.fold_in(own, 4), (count // 2,), 0, 1 << 20) % (margin + 1)
    lengths = lengths.at[giver].add(-moved).at[sink].add(moved)
    members = jnp.searchsorted(jnp.cumsum(lengths), jnp.arange(rows * top), side="right").astype(jnp.int32)
    table = members.reshape(top, rows).T
    table = table[jax.random.permutation(jax.random.fold_in(own, 1), rows)]
    turn = jax.random.randint(jax.random.fold_in(own, 2), (rows, 1), 0, top)
    return jnp.take_along_axis(table, (jnp.arange(top)[None, :] + turn) % top, axis=1)


def load_shares(number_of, total, most, lean, full):
    weights = [(1 << 20) // math.isqrt(rank ** lean) + 1 for rank in range(1, number_of + 1)]
    largest = most if full else min(most, max(-(-total // number_of), total * weights[0] // sum(weights)))
    least = 1 if total - largest >= number_of - 1 else 0
    given, spare = [largest] + [least] * (number_of - 1), total - largest - least * (number_of - 1)
    while spare > 0:
        movable = [i for i in range(1, number_of) if given[i] < largest] or [i for i in range(1, number_of) if given[i] < most]
        whole, budget = sum([weights[i] for i in movable]), spare
        for i in movable:
            more = min(most - given[i], max(1, budget * weights[i] // whole), spare)
            given[i] = given[i] + more
            spare = spare - more
    return np.array(given)


def normal_values(rng, extent, scale, bound, pieces=(), kind=jnp.bfloat16):
    drawn = scale * jax.random.normal(rng, extent, jnp.float32)
    if pieces:
        drawn = drawn * level_of(rng, extent, pieces, -0.22, 0.18)
    return jnp.clip(drawn, -bound, bound).astype(kind)


def setup_inputs(seed: int = 0) -> dict:
    key_of = jax.random.split(jax.random.key(seed), 9)
    slot_grads = normal_values(key_of[0], (SLOTS, FF, D), 1.0, 6.0, ((0, 128),))
    weights = normal_values(key_of[1], (EXPERTS, FF, D), FF ** -0.5, 0.21875, ((1, 32), (2, 4)))
    moment = normal_values(key_of[2], (EXPERTS, FF, D), 0.3, 2.0, ((1, 32), (2, 4)), jnp.float32)
    second = jnp.clip(jnp.exp(math.log(1.0) - 4.6051702 * jax.random.uniform(key_of[3], (EXPERTS, FF, D), jnp.float32) ** level_of(key_of[3], (EXPERTS, FF, D), ((1, 32), (2, 4)), -0.2, 0.2)), 0.01, 1.0)
    counts_old = draw_counts_old(jax.random.fold_in(key_of[8], 71), 0)
    counts_new = draw_counts_new(jax.random.fold_in(key_of[8], 71), 0)
    inputs = normal_values(key_of[6], (TOKENS, FF), 1.0, 6.0, ((0, 128),))
    row_slot_keys = jax.random.split(jax.random.fold_in(key_of[7], 1), TOKENS // TOK_DEV)
    row_slot_turns = jax.random.permutation(jax.random.fold_in(key_of[7], 3), TOKENS // TOK_DEV)
    row_slot = jax.vmap(lambda own, number: deal_out(jax.random.fold_in(key_of[7], 2), own, number, TOK_DEV, SLOTS, 1, CAP, 2))(row_slot_keys, row_slot_turns).reshape((TOKENS, 1))
    return dict(slot_grads=slot_grads, weights=weights, moment=moment, second=second, counts_old=counts_old, counts_new=counts_new, inputs=inputs, row_slot=row_slot)


def slot_table(counts, n_slots):
    bounds = jnp.cumsum(counts).astype(jnp.int32)
    slots = jnp.arange(n_slots, dtype=jnp.int32)
    return lax.optimization_barrier(jnp.sum((bounds[None, :] <= slots[:, None]).astype(jnp.int32), axis=1)).astype(jnp.int32)

def reference(slot_grads, weights, moment, second, counts_old, counts_new, inputs, row_slot):
    n_slots = slot_grads.shape[0]
    experts = weights.shape[0]
    table_old = slot_table(counts_old, n_slots)
    table_new = slot_table(counts_new, n_slots)
    grads = jax.ops.segment_sum(slot_grads.astype(jnp.float32), table_old, num_segments=experts)
    new_moment = 0.9 * moment + 0.1 * grads
    new_second = 0.95 * second + 0.05 * grads * grads
    bias_one = 1.0 - 0.9 ** 10
    bias_two = 1.0 - 0.95 ** 10
    update = 0.001 * (new_moment / bias_one) / (jnp.sqrt(new_second / bias_two) + 1e-08)
    new_weights = (weights.astype(jnp.float32) - update).astype(jnp.bfloat16)
    slots = row_slot[:, 0].astype(jnp.int32)
    order = jnp.argsort(slots, stable=True).astype(jnp.int32)
    per_slot = lax.optimization_barrier(jnp.sum((slots[None, :] == jnp.arange(n_slots, dtype=jnp.int32)[:, None]).astype(jnp.int32), axis=1))
    starts = (jnp.cumsum(per_slot) - per_slot).astype(jnp.int32)
    reach = 2 * TOK_DEV
    total_rows = inputs.shape[0]

    def one_slot(g, acc):
        offsets = jnp.arange(reach, dtype=jnp.int32)
        valid = offsets < per_slot[g]
        rows = order[jnp.minimum(starts[g] + offsets, total_rows - 1)]
        block = jnp.where(valid[:, None], inputs[rows], jnp.zeros((), jnp.bfloat16))
        result = jnp.dot(block, new_weights[table_new[g]], preferred_element_type=jnp.float32)
        result = jnp.where(valid[:, None], result, jnp.zeros((), jnp.float32))
        return acc.at[rows].add(result)
    acc = lax.fori_loop(0, n_slots, one_slot, jnp.zeros((total_rows, weights.shape[2]), jnp.float32))
    return (new_weights, new_moment, new_second, acc.astype(jnp.bfloat16))
```

```python
import jax
import jax.numpy as jnp
from jax import lax
from jax.experimental import pallas as pl
from jax.experimental.pallas import tpu as pltpu
from jax.sharding import PartitionSpec as P

ALL = ("slot", "own")
F32 = jnp.float32
BF16 = jnp.bfloat16
MIB = 1 << 20


def exchange(array):
    return lax.all_to_all(array, ALL, split_axis=0, concat_axis=0, tiled=True)


def rank_column(target):
    rows = target.shape[0]
    at = lax.broadcasted_iota(jnp.int32, (rows, rows), 0)
    to = lax.broadcasted_iota(jnp.int32, (rows, rows), 1)
    across = jnp.sum(jnp.where(at == to, target, 0), axis=0, keepdims=True)
    same = target == across
    return at, to, across, same


def pack_kernel(slot_ref, grads_ref, inputs_ref, out_ref, place_ref, *, groups, owners, hidden_rows, wide):
    parts = hidden_rows // 8

    @pl.when(pl.program_id(0) == 0)
    def _():
        target = slot_ref[...]
        at, to, across, same = rank_column(target)
        rank = jnp.sum(jnp.where(same & (at < to), 1, 0), axis=0, keepdims=True)
        place_ref[...] = jnp.broadcast_to(across * 8 + rank, place_ref.shape)

    for q in range(groups):
        for z in range(owners):
            for i in range(parts):
                out_ref[q * owners + z, :, i * wide : (i + 1) * wide] = grads_ref[
                    0, pl.ds(q * hidden_rows + 8 * i, 8), z * wide : (z + 1) * wide
                ]
    there = groups * owners * 8
    half = inputs_ref.shape[1] // 2
    tokens = inputs_ref.shape[0]
    row = lax.broadcasted_iota(jnp.int32, (there, tokens), 0)
    line = pl.program_id(0) * there + row - (row & 4)
    chosen = jnp.where(line == place_ref[0:1, :], 1.0, 0.0).astype(BF16)
    low = jnp.dot(chosen, inputs_ref[:, :half], preferred_element_type=F32)
    high = jnp.dot(chosen, inputs_ref[:, half:], preferred_element_type=F32)
    upper = (lax.broadcasted_iota(jnp.int32, (there, half), 0) & 4) > 0
    rows = jnp.where(upper, high, low).reshape(groups * owners, 8, half)
    out_ref[:, :, parts * wide :] = rows.astype(BF16)


def adam_kernel(
    table_ref, pieces_ref, weights_ref, moment_ref, second_ref, nw_ref, nm_ref, nv_ref, hosted_ref, *, block, wide
):
    parts = weights_ref.shape[1] // 8
    last = pieces_ref.shape[0] - 1
    bias_one = 1.0 - 0.9**10
    bias_two = 1.0 - 0.95**10
    base = pl.program_id(0) * block

    def one(k, carry):
        e = base + k
        start = table_ref[0, e]
        count = table_ref[1, e]
        start_new = table_ref[2, e]
        count_new = table_ref[3, e]
        for i in range(parts):
            cols = slice(i * wide, (i + 1) * wide)
            rows = slice(8 * i, 8 * i + 8)
            g = pieces_ref[start, :, cols].astype(F32)
            for j in range(1, 4):
                piece = pieces_ref[jnp.minimum(start + j, last), :, cols].astype(F32)
                g = g + jnp.where(count > j, piece, 0.0)
            nm = 0.9 * moment_ref[k, rows, :] + 0.1 * g
            nv = 0.95 * second_ref[k, rows, :] + 0.05 * g * g
            nm_ref[k, rows, :] = nm
            nv_ref[k, rows, :] = nv
            update = 0.001 * (nm / bias_one) / (jnp.sqrt(nv / bias_two) + 1e-08)
            nw = (weights_ref[k, rows, :].astype(F32) - update).astype(BF16)
            nw_ref[k, rows, :] = nw
            for j in range(4):

                @pl.when(j < count_new)
                def _():
                    hosted_ref[start_new + j, :, cols] = nw

        return carry

    lax.fori_loop(0, block, one, 0)


def lhs_kernel(rows_ref, lhs_ref):
    half = rows_ref.shape[2]
    wide = rows_ref[...].astype(F32).reshape(rows_ref.shape[0] // 2, 2, 8, half)
    even = wide[:, 0]
    odd = wide[:, 1]
    first = lax.broadcasted_iota(jnp.int32, even.shape, 1) < 4
    low = jnp.where(first, even, pltpu.roll(odd, 4, 1))
    high = jnp.where(first, pltpu.roll(even, 4, 1), odd)
    rows = even.shape[0] * 8
    lhs_ref[:, :half] = low.reshape(rows, half).astype(BF16)
    lhs_ref[:, half:] = high.reshape(rows, half).astype(BF16)


def product_kernel(landed_ref, lhs_ref, out_ref, matrix_ref, *, owners, wide, step):
    parts = landed_ref.shape[2] // wide
    groups = landed_ref.shape[0] // owners
    for s in range(groups):
        for z in range(owners):
            for i in range(parts):
                matrix_ref[(s * parts + i) * 8 : (s * parts + i) * 8 + 8, z * wide : (z + 1) * wide] = landed_ref[
                    s * owners + z, :, i * wide : (i + 1) * wide
                ]
    half = matrix_ref.shape[1] // 2
    devices = out_ref.shape[0]
    lhs = lhs_ref[...]
    for n in range(0, half, step):
        a = jnp.dot(lhs, matrix_ref[:, n : n + step], preferred_element_type=F32)
        b = jnp.dot(lhs, matrix_ref[:, half + n : half + n + step], preferred_element_type=F32)
        a = a.reshape(devices // 2, 8, step)
        b = b.reshape(devices // 2, 8, step)
        first = lax.broadcasted_iota(jnp.int32, a.shape, 1) < 4
        even = jnp.where(first, a, pltpu.roll(b, 4, 1)).astype(BF16)
        odd = jnp.where(first, pltpu.roll(a, 4, 1), b).astype(BF16)
        out_ref[:, :, n : n + step] = jnp.stack([even, odd], axis=1).reshape(devices, 8, step)


def gather_kernel(slot_ref, returned_ref, out_ref):
    target = slot_ref[...]
    at, to, _, same = rank_column(target)
    rank = jnp.sum(jnp.where(same & (to < at), 1, 0), axis=1, keepdims=True)
    place = target * 8 + rank
    tokens = target.shape[0]
    lines, half = returned_ref.shape
    column = lax.broadcasted_iota(jnp.int32, (tokens, lines), 1)
    for h in range(2):
        chosen = jnp.where(column == place + 4 * h, 1.0, 0.0).astype(BF16)
        out_ref[:, h * half : (h + 1) * half] = jnp.dot(
            chosen, returned_ref[...], preferred_element_type=F32
        ).astype(BF16)


def params(mib=48):
    return pltpu.CompilerParams(vmem_limit_bytes=mib * MIB)


def body(slot_grads, weights, moment, second, counts_old, counts_new, inputs, row_slot):
    owners = lax.axis_size("own")
    devices = lax.axis_size("slot") * owners
    experts, rows_here, cols_here = weights.shape
    hidden, width = slot_grads.shape[1:]
    tokens = inputs.shape[0]
    parts = rows_here // 8
    half = hidden // 2
    span = parts * cols_here
    whole = lambda *shape: pl.BlockSpec(shape, lambda *_: (0,) * len(shape))

    steps = 8
    groups = devices // owners // steps
    packed = pl.pallas_call(
        lambda *refs: pack_kernel(*refs, groups=groups, owners=owners, hidden_rows=rows_here, wide=cols_here),
        out_shape=jax.ShapeDtypeStruct((devices, 8, span + half), BF16),
        grid=(steps,),
        in_specs=[
            whole(tokens, 1),
            pl.BlockSpec((1, groups * rows_here, width), lambda k: (0, k, 0)),
            whole(tokens, hidden),
        ],
        out_specs=pl.BlockSpec((groups * owners, 8, span + half), lambda k: (k, 0, 0)),
        scratch_shapes=[pltpu.VMEM((8, tokens), jnp.int32)],
        compiler_params=params(),
        name="pack",
    )(row_slot, slot_grads, inputs)
    arrived = exchange(packed)

    table = jnp.stack(
        [jnp.cumsum(counts_old) - counts_old, counts_old, jnp.cumsum(counts_new) - counts_new, counts_new]
    ).astype(jnp.int32)
    block = 8
    state = pl.BlockSpec((block, rows_here, cols_here), lambda k, *_: (k, 0, 0))
    new_weights, new_moment, new_second, hosted = pl.pallas_call(
        lambda *refs: adam_kernel(*refs, block=block, wide=cols_here),
        out_shape=(
            jax.ShapeDtypeStruct(weights.shape, BF16),
            jax.ShapeDtypeStruct(moment.shape, F32),
            jax.ShapeDtypeStruct(second.shape, F32),
            jax.ShapeDtypeStruct((devices, 8, span), BF16),
        ),
        grid_spec=pltpu.PrefetchScalarGridSpec(
            num_scalar_prefetch=1,
            grid=(experts // block,),
            in_specs=[whole(devices, 8, span), state, state, state],
            out_specs=(state, state, state, whole(devices, 8, span)),
        ),
        compiler_params=params(),
        name="adam",
    )(table, arrived, weights, moment, second)
    landed = exchange(hosted)

    lhs = pl.pallas_call(
        lhs_kernel,
        out_shape=jax.ShapeDtypeStruct((devices * 4, hidden), BF16),
        grid=(1,),
        in_specs=[pl.BlockSpec((devices, 8, half), lambda k: (0, 0, span // half))],
        out_specs=whole(devices * 4, hidden),
        compiler_params=params(),
        name="lhs",
    )(arrived)
    produced = pl.pallas_call(
        lambda *refs: product_kernel(*refs, owners=owners, wide=cols_here, step=256),
        out_shape=jax.ShapeDtypeStruct((devices, 8, width // 2), BF16),
        grid=(1,),
        in_specs=[whole(devices, 8, span), whole(devices * 4, hidden)],
        out_specs=whole(devices, 8, width // 2),
        scratch_shapes=[pltpu.VMEM((hidden, width), BF16)],
        compiler_params=params(),
        name="product",
    )(landed, lhs)
    returned = exchange(produced)

    outputs = pl.pallas_call(
        gather_kernel,
        out_shape=jax.ShapeDtypeStruct((tokens, width), BF16),
        grid=(1,),
        in_specs=[whole(tokens, 1), whole(devices * 8, width // 2)],
        out_specs=whole(tokens, width),
        compiler_params=params(),
        name="gather",
    )(row_slot, returned.reshape(devices * 8, width // 2))
    return (new_weights, new_moment, new_second, outputs)


def solution(mesh):
    placed = (
        P(ALL, None, None),
        P(None, "slot", "own"),
        P(None, "slot", "own"),
        P(None, "slot", "own"),
        P(),
        P(),
        P(ALL, None),
        P(ALL, None),
    )
    return jax.shard_map(
        body,
        mesh=mesh,
        in_specs=placed,
        out_specs=(
            P(None, "slot", "own"),
            P(None, "slot", "own"),
            P(None, "slot", "own"),
            P(ALL, None),
        ),
        check_vma=False,
    )
```
